32 devices in a mesh: grp: 2 (over y), pipe: 8 (over z, x), head: 2 (over core).
Axes of the slice: x: 2, y: 2, z: 4, core: 2. Of those that a mesh axis runs over, the one named last changes fastest.
Arguments:
- queries: bfloat16 [512, 64, 128], P(('grp', 'pipe'), 'head'), parts along dimension 0, may hold values from -10 to 10
- slice_own_keys: bfloat16 [512, 4, 128], P(('grp', 'pipe'), 'head'), parts along dimension 0, may hold values from -6 to 6
- slice_own_values: bfloat16 [512, 4, 128], P(('grp', 'pipe'), 'head'), parts along dimension 0, may hold values from -6 to 6
- cache_keys: bfloat16 [1664, 4, 128], P(('grp', 'pipe'), 'head'), parts along dimension 0, may hold values from -8 to 8
- context_value_rows: bfloat16 [1664, 4, 128], P(('grp', 'pipe'), 'head'), parts along dimension 0, may hold values from -6 to 6
- prefix_len: int32 [16], P('grp'), parts along dimension 0, may hold values from 1 to 832, as said below
Outputs:
- advanced: bfloat16 [512, 64, 128], P(('grp', 'pipe'), 'head'), parts along dimension 0
The draws below stay inside these ranges and needn't reach their ends.
There are 2 independent parts, one for each index of `grp`. The reference program is written for one: setup_inputs(seed, part) draws one part's arguments, and reference() takes and returns one part's arrays. A program takes and returns all parts, laid end to end along the dimension named above; each array names one. Nothing has to cross between parts.
Inputs may be any that keep to these rules, and one draw needn't show every extreme that they name: prefix_len[p] lies in ((8 - 1 - p) * 104, (8 - p) * 104]; prefix_len[0] is 832 and the last section's is 1.
All inputs are finite; a program needn't handle non-finite values.
Results may differ from the reference program's by a relative error of at most 0.012.
Values may be sent and summed in bfloat16 or wider, within the bound.
No kernel may reach another device: no remote copies, remote signals or barrier semaphores. Data moves between devices by JAX's collectives and lax.ppermute only.
A program may use at most 64 MiB of HBM per device.

```python
import math
import jax
import jax.numpy as jnp
from jax import lax

HQ = 64
KEY_VALUE_HEADS = 4
HEAD_DIMENSION = 128
SLICE = 32
BLK = 104
QUERY_TOKENS = 256
CONTEXT_SPAN = 832


def draw_queries(key, part):
    complete_shape = (QUERY_TOKENS, HQ, HEAD_DIMENSION)
    scale_factors = jnp.exp(jax.random.uniform(jax.random.fold_in(key, 12), (QUERY_TOKENS, HQ, 1), jnp.float32, math.log(0.2), math.log(2.0)))
    noise_draw = jax.random.normal(jax.random.fold_in(key, 11), complete_shape, jnp.float32)
    drawn = jnp.clip(noise_draw * scale_factors, -10.0, 10.0)
    return drawn.astype(jnp.bfloat16)


def draw_cache_keys(key, part):
    complete_shape = (CONTEXT_SPAN, KEY_VALUE_HEADS, HEAD_DIMENSION)
    scale_factors = jnp.exp(jax.random.uniform(jax.random.fold_in(key, 14), (CONTEXT_SPAN, KEY_VALUE_HEADS, 1), jnp.float32, math.log(0.35), math.log(3.5)))
    noise_draw = jax.random.normal(jax.random.fold_in(key, 13), complete_shape, jnp.float32)
    drawn = jnp.clip(noise_draw * scale_factors, -8.0, 8.0)
    return drawn.astype(jnp.bfloat16)


def draw_prefix_len(key, part):
    sections = CONTEXT_SPAN // BLK
    section_index = jnp.arange(sections)
    jitter = jax.random.randint(jax.random.fold_in(key, 21), (sections,), 1, BLK + 1)
    jitter = jnp.where(section_index == 0, BLK, jnp.where(section_index == sections - 1, 1, jitter))
    return ((sections - 1 - section_index) * BLK + jitter).astype(jnp.int32)


def steps_of(own_key, shape, split, smallest, top_value):
    factor_of, own = 1.0, jax.random.fold_in(own_key, 6)
    for dim, blocks in split:
        draws = jnp.exp(jax.random.uniform(jax.random.fold_in(own, dim), (blocks,), jnp.float32, smallest / len(split), top_value / len(split)))
        factor_of = factor_of * jnp.repeat(draws, shape[dim] // blocks).reshape([-1 if axis == dim else 1 for axis in range(len(shape))])
    return factor_of


def scatter_about(own_key, dims, width, most, cuts=(), held_as=jnp.bfloat16):
    result = width * jax.random.normal(own_key, dims, jnp.float32)
    if cuts:
        result = result * steps_of(own_key, dims, cuts, -0.22, 0.18)
    return jnp.clip(result, -most, most).astype(held_as)


def setup_inputs(seed: int = 0, part: int = 0) -> dict:
    key_of = jax.random.split(jax.random.key(seed), 7)
    part_keys = jax.random.split(jax.random.fold_in(key_of[6], part), 7)
    return {
        "queries": draw_queries(jax.random.fold_in(jax.random.fold_in(key_of[6], part), 71), part),
        "slice_own_keys": scatter_about(part_keys[1], (QUERY_TOKENS, KEY_VALUE_HEADS, HEAD_DIMENSION), 1.0, 6.0, ((0, 8), (1, 2))),
        "slice_own_values": scatter_about(part_keys[2], (QUERY_TOKENS, KEY_VALUE_HEADS, HEAD_DIMENSION), 1.0, 6.0, ((0, 8), (1, 2))),
        "cache_keys": draw_cache_keys(jax.random.fold_in(jax.random.fold_in(key_of[6], part), 71), part),
        "context_value_rows": scatter_about(part_keys[4], (CONTEXT_SPAN, KEY_VALUE_HEADS, HEAD_DIMENSION), 1.0, 6.0, ((0, 8), (1, 2))),
        "prefix_len": draw_prefix_len(jax.random.fold_in(jax.random.fold_in(key_of[6], part), 71), part),
    }


def reference(queries, slice_own_keys, slice_own_values, cache_keys, context_value_rows, prefix_len):
    token_count, head_count, head_width = queries.shape
    groups = slice_own_keys.shape[1]
    per_group = head_count // groups
    sections = token_count // SLICE
    context = cache_keys.shape[0]
    factor = 1.0 / math.sqrt(head_width)
    cached_keys = cache_keys.astype(jnp.float32)
    cached_values = context_value_rows.astype(jnp.float32)

    def section_output(pieces):
        query_block, key_block, value_block, prefix = pieces
        all_keys = jnp.concatenate([cached_keys, key_block.astype(jnp.float32)], axis=0)
        all_values = jnp.concatenate([cached_values, value_block.astype(jnp.float32)], axis=0)
        scores = jnp.einsum('sghd,kgd->gkhs', query_block.astype(jnp.float32), all_keys) * factor
        key_index = lax.broadcasted_iota(jnp.int32, (1, context + SLICE, 1, SLICE), 1)
        row_index = lax.broadcasted_iota(jnp.int32, (1, context + SLICE, 1, SLICE), 3)
        visible = jnp.where(key_index < context, key_index < prefix, key_index - context <= row_index)
        row_max = lax.optimization_barrier(jnp.max(jnp.where(visible, scores, -1e+30), axis=1))
        weights = jnp.where(visible, jnp.exp(scores - row_max[:, None]), 0.0)
        row_sum = lax.optimization_barrier(jnp.sum(weights, axis=1))
        rounded = lax.optimization_barrier(weights.astype(jnp.bfloat16)).astype(jnp.float32)
        weighted = jnp.einsum('gkhs,kgd->sghd', rounded, all_values)
        attended = weighted / jnp.transpose(row_sum, (2, 0, 1))[..., None]
        return attended.astype(jnp.bfloat16).reshape(SLICE, head_count, head_width)
    outputs = lax.map(section_output, (queries.reshape(sections, SLICE, groups, per_group, head_width), slice_own_keys.reshape(sections, SLICE, groups, head_width), slice_own_values.reshape(sections, SLICE, groups, head_width), prefix_len))
    return jnp.roll(outputs, 1, axis=0).reshape(token_count, head_count, head_width)
```

```python
import functools
import math

import jax
import jax.numpy as jnp
from jax import lax
from jax.experimental import pallas as pl
from jax.experimental.pallas import tpu as pltpu
from jax.sharding import PartitionSpec as P

floor_value = -1e30
unrolled_sections = 16


def swapped(value, axis, mask):
    count = lax.axis_size(axis)
    return lax.ppermute(value, axis, [(source, source ^ mask) for source in range(count)])


def passed_along(value, axis, steps):
    count = lax.axis_size(axis)
    pairs = [(source, (source + steps) % count) for source in range(count)]
    return lax.ppermute(value, axis, pairs)


def attend_kernel(factor, groups, prefix_ref, query_ref, own_ref, *refs):
    block_refs, out_ref = refs[:-1], refs[-1]
    sections = len(block_refs)
    own_index = lax.axis_index("pipe")
    prefix = prefix_ref[lax.rem(own_index + sections - 1, sections)]
    slice_rows, head_count, head_width = query_ref.shape
    per_group = head_count // groups
    block_rows = block_refs[0].shape[1]
    rows = slice_rows * per_group
    key_index = lax.broadcasted_iota(jnp.int32, (rows, slice_rows), 1)
    row_index = lax.broadcasted_iota(jnp.int32, (rows, slice_rows), 0) // per_group
    position = lax.broadcasted_iota(jnp.int32, (1, block_rows), 1)
    contract = (((1,), (1,)), ((), ()))
    for group in range(groups):
        heads = pl.ds(group * per_group, per_group)
        query = query_ref[:, heads, :].reshape(rows, head_width)
        scores = lax.dot_general(
            query, own_ref[group], contract, preferred_element_type=jnp.float32
        )
        tiles = [(jnp.where(key_index <= row_index, scores, floor_value), own_ref)]
        for index, block_ref in enumerate(block_refs):
            scores = lax.dot_general(
                query, block_ref[group], contract, preferred_element_type=jnp.float32
            )
            first_key = lax.bitwise_xor(own_index, index) * block_rows
            bias = jnp.where(position < prefix - first_key, 0.0, floor_value)
            tiles.append((scores + bias, block_ref))
        row_max = functools.reduce(
            jnp.maximum, [jnp.max(scores, axis=1, keepdims=True) for scores, _ in tiles]
        )
        total = jnp.zeros((rows, 1), jnp.float32)
        weighted = jnp.zeros((rows, head_width), jnp.float32)
        for scores, value_ref in tiles:
            weights = jnp.exp((scores - row_max) * factor)
            total += jnp.sum(weights, axis=1, keepdims=True)
            weighted += jnp.dot(
                weights.astype(jnp.bfloat16),
                value_ref[groups + group],
                preferred_element_type=jnp.float32,
            )
        out_ref[:, heads, :] = (
            (weighted / total).astype(jnp.bfloat16).reshape(slice_rows, per_group, head_width)
        )


def block_scores(grouped, key_block, factor):
    return (
        jnp.einsum("sghd,kgd->gkhs", grouped, key_block, preferred_element_type=jnp.float32)
        * factor
    )


def to_rows(statistic):
    return jnp.transpose(statistic, (2, 0, 1))[..., None]


def absorb(running, scores, value_block, visible):
    weighted, running_max, running_sum = running
    block_max = jnp.max(jnp.where(visible, scores, floor_value), axis=1)
    new_max = jnp.maximum(running_max, block_max)
    weights = jnp.where(visible, jnp.exp(scores - new_max[:, None]), 0.0)
    rescale = jnp.exp(running_max - new_max)
    added = jnp.einsum(
        "gkhs,kgd->sghd",
        weights.astype(jnp.bfloat16),
        value_block,
        preferred_element_type=jnp.float32,
    )
    return (
        weighted * to_rows(rescale) + added,
        new_max,
        running_sum * rescale + jnp.sum(weights, axis=1),
    )


def cache_range(
    running, grouped, whole_keys, whole_values, start_key, stop_key, block_rows, factor
):

    def absorb_block(block_index, carried):
        first_key = block_index * block_rows
        key_block = lax.dynamic_slice_in_dim(whole_keys, first_key, block_rows, 0)
        value_block = lax.dynamic_slice_in_dim(whole_values, first_key, block_rows, 0)
        position = first_key + lax.broadcasted_iota(jnp.int32, (1, block_rows, 1, 1), 1)
        visible = (position >= start_key) & (position < stop_key)
        return absorb(carried, block_scores(grouped, key_block, factor), value_block, visible)

    return lax.fori_loop(
        start_key // block_rows, (stop_key + block_rows - 1) // block_rows, absorb_block, running
    )


def gathered_shards(
    queries, slice_own_keys, slice_own_values, cache_keys, context_value_rows, prefix_len
):
    slice_rows, head_count, head_width = queries.shape
    groups = slice_own_keys.shape[1]
    per_group = head_count // groups
    grouped = queries.reshape(slice_rows, groups, per_group, head_width)
    factor = 1.0 / math.sqrt(head_width)
    initial = (
        jnp.zeros((slice_rows, groups, per_group, head_width), jnp.float32),
        jnp.full((groups, per_group, slice_rows), floor_value, jnp.float32),
        jnp.zeros((groups, per_group, slice_rows), jnp.float32),
    )
    key_index = lax.broadcasted_iota(jnp.int32, (1, slice_rows, 1, slice_rows), 1)
    row_index = lax.broadcasted_iota(jnp.int32, (1, slice_rows, 1, slice_rows), 3)
    running = absorb(
        initial,
        block_scores(grouped, slice_own_keys, factor),
        slice_own_values,
        key_index <= row_index,
    )
    whole_keys = lax.all_gather(cache_keys, "pipe", axis=0, tiled=True)
    whole_values = lax.all_gather(context_value_rows, "pipe", axis=0, tiled=True)
    block_rows = math.gcd(whole_keys.shape[0], 512)
    own_prefix = prefix_len[lax.axis_index("pipe")]
    weighted, _, running_sum = cache_range(
        running, grouped, whole_keys, whole_values, 0, own_prefix, block_rows, factor
    )
    result = (weighted / to_rows(running_sum)).astype(jnp.bfloat16).reshape(queries.shape)
    return passed_along(result, "pipe", 1)


def packed(keys, values):
    return jnp.concatenate([jnp.transpose(keys, (1, 0, 2)), jnp.transpose(values, (1, 0, 2))])


def swapped_shards(
    queries, slice_own_keys, slice_own_values, cache_keys, context_value_rows, prefix_len
):
    slice_rows, head_count, head_width = queries.shape
    groups = slice_own_keys.shape[1]
    sections = lax.axis_size("pipe")

    block = packed(cache_keys, context_value_rows)
    own = packed(slice_own_keys, slice_own_values)
    blocks = {0: block}
    query = passed_along(queries, "pipe", 1)
    for mask in range(sections - 2, 0, -2):
        blocks[mask] = swapped(block, "pipe", mask)
    own = passed_along(own, "pipe", 1)
    for mask in range(0, sections, 2):
        blocks[mask + 1] = swapped(blocks[mask], "pipe", 1)
    order = sorted(blocks)
    vmem = pl.BlockSpec(memory_space=pltpu.VMEM)
    return pl.pallas_call(
        functools.partial(attend_kernel, 1.0 / math.sqrt(head_width), groups),
        out_shape=jax.ShapeDtypeStruct(queries.shape, jnp.bfloat16),
        in_specs=[pl.BlockSpec(memory_space=pltpu.SMEM)] + [vmem] * (2 + sections),
        out_specs=vmem,
        compiler_params=pltpu.CompilerParams(vmem_limit_bytes=24 << 20),
        name="attend",
    )(prefix_len, query, own, *[blocks[mask] for mask in order])


def solution(mesh):
    sections = mesh.shape["pipe"]
    unrolled = sections <= unrolled_sections and sections & (sections - 1) == 0
    shards = swapped_shards if unrolled else gathered_shards
    in_specs = (
        P(("grp", "pipe"), "head", None),
        P(("grp", "pipe"), "head", None),
        P(("grp", "pipe"), "head", None),
        P(("grp", "pipe"), "head", None),
        P(("grp", "pipe"), "head", None),
        P("grp"),
    )
    out_specs = P(("grp", "pipe"), "head", None)
    return jax.shard_map(shards, mesh=mesh, in_specs=in_specs, out_specs=out_specs, check_vma=False)
```

```python
import functools
import math

import jax
import jax.numpy as jnp
from jax import lax
from jax.experimental import pallas as pl
from jax.experimental.pallas import tpu as pltpu
from jax.sharding import PartitionSpec as P


floor_value = -1e30
unrolled_sections = 16


def swapped(value, axis, mask):
    count = lax.axis_size(axis)
    return lax.ppermute(value, axis, [(source, source ^ mask) for source in range(count)])


def passed_along(value, axis, steps):
    count = lax.axis_size(axis)
    pairs = [(source, (source + steps) % count) for source in range(count)]
    return lax.ppermute(value, axis, pairs)


def attend_kernel(factor, groups, prefix_ref, query_ref, own_ref, *refs):
    block_refs, out_ref = refs[:-1], refs[-1]
    sections = len(block_refs)
    own_index = lax.axis_index("pipe")
    prefix = prefix_ref[lax.rem(own_index + sections - 1, sections)]
    slice_rows, head_count, head_width = query_ref.shape
    per_group = head_count // groups
    block_rows = block_refs[0].shape[1]
    rows = slice_rows * per_group
    key_index = lax.broadcasted_iota(jnp.int32, (rows, slice_rows), 1)
    row_index = lax.broadcasted_iota(jnp.int32, (rows, slice_rows), 0) // per_group
    position = lax.broadcasted_iota(jnp.int32, (1, block_rows), 1)
    contract = (((1,), (1,)), ((), ()))
    for group in range(groups):
        heads = pl.ds(group * per_group, per_group)
        query = query_ref[:, heads, :].reshape(rows, head_width)
        scores = lax.dot_general(
            query, own_ref[group], contract, preferred_element_type=jnp.float32
        )
        tiles = [(jnp.where(key_index <= row_index, scores, floor_value), own_ref)]
        for index, block_ref in enumerate(block_refs):
            scores = lax.dot_general(
                query, block_ref[group], contract, preferred_element_type=jnp.float32
            )
            first_key = lax.bitwise_xor(own_index, index) * block_rows
            bias = jnp.where(position < prefix - first_key, 0.0, floor_value)
            tiles.append((scores + bias, block_ref))
        row_max = functools.reduce(
            jnp.maximum, [jnp.max(scores, axis=1, keepdims=True) for scores, _ in tiles]
        )
        total = jnp.zeros((rows, 1), jnp.float32)
        weighted = jnp.zeros((rows, head_width), jnp.float32)
        for scores, value_ref in tiles:
            weights = jnp.exp((scores - row_max) * factor)
            total += jnp.sum(weights, axis=1, keepdims=True)
            weighted += jnp.dot(
                weights.astype(jnp.bfloat16),
                value_ref[groups + group],
                preferred_element_type=jnp.float32,
            )
        out_ref[:, heads, :] = (
            (weighted / total).astype(jnp.bfloat16).reshape(slice_rows, per_group, head_width)
        )


def block_scores(grouped, key_block, factor):
    return (
        jnp.einsum("sghd,kgd->gkhs", grouped, key_block, preferred_element_type=jnp.float32)
        * factor
    )


def to_rows(statistic):
    return jnp.transpose(statistic, (2, 0, 1))[..., None]


def absorb(running, scores, value_block, visible):
    weighted, running_max, running_sum = running
    block_max = jnp.max(jnp.where(visible, scores, floor_value), axis=1)
    new_max = jnp.maximum(running_max, block_max)
    weights = jnp.where(visible, jnp.exp(scores - new_max[:, None]), 0.0)
    rescale = jnp.exp(running_max - new_max)
    added = jnp.einsum(
        "gkhs,kgd->sghd",
        weights.astype(jnp.bfloat16),
        value_block,
        preferred_element_type=jnp.float32,
    )
    return (
        weighted * to_rows(rescale) + added,
        new_max,
        running_sum * rescale + jnp.sum(weights, axis=1),
    )


def cache_range(
    running, grouped, whole_keys, whole_values, start_key, stop_key, block_rows, factor
):

    def absorb_block(block_index, carried):
        first_key = block_index * block_rows
        key_block = lax.dynamic_slice_in_dim(whole_keys, first_key, block_rows, 0)
        value_block = lax.dynamic_slice_in_dim(whole_values, first_key, block_rows, 0)
        position = first_key + lax.broadcasted_iota(jnp.int32, (1, block_rows, 1, 1), 1)
        visible = (position >= start_key) & (position < stop_key)
        return absorb(carried, block_scores(grouped, key_block, factor), value_block, visible)

    return lax.fori_loop(
        start_key // block_rows, (stop_key + block_rows - 1) // block_rows, absorb_block, running
    )


def gathered_shards(
    queries, slice_own_keys, slice_own_values, cache_keys, context_value_rows, prefix_len
):
    slice_rows, head_count, head_width = queries.shape
    groups = slice_own_keys.shape[1]
    per_group = head_count // groups
    grouped = queries.reshape(slice_rows, groups, per_group, head_width)
    factor = 1.0 / math.sqrt(head_width)
    initial = (
        jnp.zeros((slice_rows, groups, per_group, head_width), jnp.float32),
        jnp.full((groups, per_group, slice_rows), floor_value, jnp.float32),
        jnp.zeros((groups, per_group, slice_rows), jnp.float32),
    )
    key_index = lax.broadcasted_iota(jnp.int32, (1, slice_rows, 1, slice_rows), 1)
    row_index = lax.broadcasted_iota(jnp.int32, (1, slice_rows, 1, slice_rows), 3)
    running = absorb(
        initial,
        block_scores(grouped, slice_own_keys, factor),
        slice_own_values,
        key_index <= row_index,
    )
    whole_keys = lax.all_gather(cache_keys, "pipe", axis=0, tiled=True)
    whole_values = lax.all_gather(context_value_rows, "pipe", axis=0, tiled=True)
    block_rows = math.gcd(whole_keys.shape[0], 512)
    own_prefix = prefix_len[lax.axis_index("pipe")]
    weighted, _, running_sum = cache_range(
        running, grouped, whole_keys, whole_values, 0, own_prefix, block_rows, factor
    )
    result = (weighted / to_rows(running_sum)).astype(jnp.bfloat16).reshape(queries.shape)
    return passed_along(result, "pipe", 1)


def gather_order(sections):
    masks = range(1, sections)
    return sorted(masks, key=lambda mask: (mask.bit_count(), -mask))


def packed(keys, values):
    return jnp.concatenate([jnp.transpose(keys, (1, 0, 2)), jnp.transpose(values, (1, 0, 2))])


def swapped_shards(
    queries, slice_own_keys, slice_own_values, cache_keys, context_value_rows, prefix_len
):
    _, _, head_width = queries.shape
    groups = slice_own_keys.shape[1]
    sections = lax.axis_size("pipe")

    block = packed(cache_keys, context_value_rows)
    own = packed(slice_own_keys, slice_own_values)
    blocks = {0: block}
    for mask in gather_order(sections):
        blocks[mask] = swapped(blocks[mask & (mask - 1)], "pipe", mask & -mask)
    query = passed_along(queries, "pipe", 1)
    own = passed_along(own, "pipe", 1)
    order = sorted(blocks)
    vmem = pl.BlockSpec(memory_space=pltpu.VMEM)
    return pl.pallas_call(
        functools.partial(attend_kernel, 1.0 / math.sqrt(head_width), groups),
        out_shape=jax.ShapeDtypeStruct(queries.shape, jnp.bfloat16),
        in_specs=[pl.BlockSpec(memory_space=pltpu.SMEM)] + [vmem] * (2 + sections),
        out_specs=vmem,
        compiler_params=pltpu.CompilerParams(vmem_limit_bytes=24 << 20),
        name="attend",
    )(prefix_len, query, own, *[blocks[mask] for mask in order])


def solution(mesh):
    sections = mesh.shape["pipe"]
    unrolled = sections <= unrolled_sections and sections & (sections - 1) == 0
    shards = swapped_shards if unrolled else gathered_shards
    in_specs = (
        P(("grp", "pipe"), "head", None),
        P(("grp", "pipe"), "head", None),
        P(("grp", "pipe"), "head", None),
        P(("grp", "pipe"), "head", None),
        P(("grp", "pipe"), "head", None),
        P("grp"),
    )
    out_specs = P(("grp", "pipe"), "head", None)
    return jax.shard_map(shards, mesh=mesh, in_specs=in_specs, out_specs=out_specs, check_vma=False)
```

```python
import functools
import math

import jax
import jax.numpy as jnp
from jax import lax
from jax.experimental import pallas as pl
from jax.experimental.pallas import tpu as pltpu
from jax.sharding import PartitionSpec as P


floor_value = -1e30
unrolled_sections = 16


def passed_along(value, axis, steps):
    count = lax.axis_size(axis)
    pairs = [(source, (source + steps) % count) for source in range(count)]
    return lax.ppermute(value, axis, pairs)


def attend_kernel(
    scale, groups, chunk, prefix_ref, even_ref, odd_ref, own_ref, *refs
):
    block_refs, out_ref = refs[:-1], refs[-1]
    own_index = lax.axis_index("pipe")
    sections = len(block_refs)
    odd = lax.rem(own_index, 2) == 1
    section = lax.rem(own_index + sections - 1, sections)
    column = lax.broadcasted_iota(jnp.int32, (1, sections), 1)
    prefix = jnp.where(column == section, prefix_ref[...].astype(jnp.float32), 0.0)
    prefix = jnp.sum(prefix, axis=1, keepdims=True).astype(jnp.int32)
    slice_rows, head_count, head_width = out_ref.shape
    per_group = head_count // groups
    block_rows = block_refs[0].shape[1]
    contract = (((1,), (1,)), ((), ()))

    def attend_blocks(masks):
        context = len(masks) * block_rows
        keys_total = context + slice_rows
        position = lax.broadcasted_iota(jnp.int32, (1, keys_total), 1)
        limit = jnp.full((1, keys_total), keys_total, jnp.int32)
        for mask in masks:
            first_key = lax.bitwise_xor(own_index, mask) * block_rows
            stop = jnp.minimum(prefix - first_key, block_rows) + mask * block_rows
            limit = jnp.where(position // block_rows == mask, stop, limit)
        bias = jnp.where(position < limit, 0.0, floor_value)
        for group in range(groups):
            heads = pl.ds(group * per_group, per_group)
            keys = jnp.concatenate(
                [block_refs[mask][group] for mask in masks] + [own_ref[group]], axis=0
            )
            values = jnp.concatenate(
                [block_refs[mask][groups + group] for mask in masks] + [own_ref[groups + group]],
                axis=0,
            )
            for first in range(0, slice_rows, chunk):
                tokens = pl.ds(first, chunk)
                rows = chunk * per_group
                query = jnp.where(odd, odd_ref[tokens, heads, :], even_ref[tokens, heads, :])
                query = query.reshape(rows, head_width)
                scores = lax.dot_general(
                    query, keys, contract, preferred_element_type=jnp.float32
                )
                key_index = lax.broadcasted_iota(jnp.int32, (rows, keys_total), 1) - context
                row_index = lax.broadcasted_iota(jnp.int32, (rows, keys_total), 0) // per_group
                scores = jnp.where(key_index <= row_index + first, scores + bias, floor_value)
                row_max = jnp.max(scores, axis=1, keepdims=True)
                weights = jnp.exp2((scores - row_max) * scale)
                total = jnp.sum(weights, axis=1, keepdims=True)
                weighted = jnp.dot(
                    weights.astype(jnp.bfloat16), values, preferred_element_type=jnp.float32
                )
                out_ref[tokens, heads, :] = (
                    (weighted / total).astype(jnp.bfloat16).reshape(chunk, per_group, head_width)
                )

    @pl.when(own_index == 0)
    def _():
        attend_blocks(range(1))

    @pl.when(own_index != 0)
    def _():
        attend_blocks(range(sections))


def attend(prefix_len, even_query, odd_query, own, blocks, groups):
    slice_rows, head_count, head_width = even_query.shape
    rows = slice_rows * head_count
    vmem = pl.BlockSpec(memory_space=pltpu.VMEM)
    keys = sum(block.shape[1] for block in blocks)
    scale = math.log2(math.e) / math.sqrt(head_width)
    return pl.pallas_call(
        functools.partial(attend_kernel, scale, groups, slice_rows),
        out_shape=jax.ShapeDtypeStruct(even_query.shape, jnp.bfloat16),
        in_specs=[vmem] * (4 + len(blocks)),
        out_specs=vmem,
        compiler_params=pltpu.CompilerParams(vmem_limit_bytes=24 << 20),
        cost_estimate=pl.CostEstimate(
            flops=4 * keys * rows * head_width,
            bytes_accessed=4 * rows * head_width,
            transcendentals=keys * rows,
        ),
        name="attend",
    )(prefix_len.reshape(1, -1), even_query, odd_query, own, *blocks)


def block_scores(grouped, key_block, factor):
    return (
        jnp.einsum("sghd,kgd->gkhs", grouped, key_block, preferred_element_type=jnp.float32)
        * factor
    )


def to_rows(statistic):
    return jnp.transpose(statistic, (2, 0, 1))[..., None]


def absorb(running, scores, value_block, visible):
    weighted, running_max, running_sum = running
    block_max = jnp.max(jnp.where(visible, scores, floor_value), axis=1)
    new_max = jnp.maximum(running_max, block_max)
    weights = jnp.where(visible, jnp.exp(scores - new_max[:, None]), 0.0)
    rescale = jnp.exp(running_max - new_max)
    added = jnp.einsum(
        "gkhs,kgd->sghd",
        weights.astype(jnp.bfloat16),
        value_block,
        preferred_element_type=jnp.float32,
    )
    return (
        weighted * to_rows(rescale) + added,
        new_max,
        running_sum * rescale + jnp.sum(weights, axis=1),
    )


def cache_range(
    running, grouped, whole_keys, whole_values, start_key, stop_key, block_rows, factor
):

    def absorb_block(block_index, carried):
        first_key = block_index * block_rows
        key_block = lax.dynamic_slice_in_dim(whole_keys, first_key, block_rows, 0)
        value_block = lax.dynamic_slice_in_dim(whole_values, first_key, block_rows, 0)
        position = first_key + lax.broadcasted_iota(jnp.int32, (1, block_rows, 1, 1), 1)
        visible = (position >= start_key) & (position < stop_key)
        return absorb(carried, block_scores(grouped, key_block, factor), value_block, visible)

    return lax.fori_loop(
        start_key // block_rows, (stop_key + block_rows - 1) // block_rows, absorb_block, running
    )


def gathered_shards(
    queries, slice_own_keys, slice_own_values, cache_keys, context_value_rows, prefix_len
):
    slice_rows, head_count, head_width = queries.shape
    groups = slice_own_keys.shape[1]
    per_group = head_count // groups
    grouped = queries.reshape(slice_rows, groups, per_group, head_width)
    factor = 1.0 / math.sqrt(head_width)
    initial = (
        jnp.zeros((slice_rows, groups, per_group, head_width), jnp.float32),
        jnp.full((groups, per_group, slice_rows), floor_value, jnp.float32),
        jnp.zeros((groups, per_group, slice_rows), jnp.float32),
    )
    key_index = lax.broadcasted_iota(jnp.int32, (1, slice_rows, 1, slice_rows), 1)
    row_index = lax.broadcasted_iota(jnp.int32, (1, slice_rows, 1, slice_rows), 3)
    running = absorb(
        initial,
        block_scores(grouped, slice_own_keys, factor),
        slice_own_values,
        key_index <= row_index,
    )
    whole_keys = lax.all_gather(cache_keys, "pipe", axis=0, tiled=True)
    whole_values = lax.all_gather(context_value_rows, "pipe", axis=0, tiled=True)
    block_rows = math.gcd(whole_keys.shape[0], 512)
    own_prefix = prefix_len[lax.axis_index("pipe")]
    weighted, _, running_sum = cache_range(
        running, grouped, whole_keys, whole_values, 0, own_prefix, block_rows, factor
    )
    result = (weighted / to_rows(running_sum)).astype(jnp.bfloat16).reshape(queries.shape)
    return passed_along(result, "pipe", 1)


def gather_plan(sections):
    every = range(sections)
    top = sections // 2

    def rank(mask):
        if mask.bit_count() > 1:
            return mask.bit_count(), -mask
        return 1, 0 if mask == top else mask

    moves = []
    for mask in sorted(range(1, sections), key=rank):
        swap = [(device, device ^ (mask & -mask)) for device in every]
        moves.append((f"m{mask}", f"m{mask & (mask - 1)}", swap))
    singles = sections.bit_length() - 1
    neighbours = [(device, device ^ 1) for device in every]
    ring = [(device, (device + 1) % sections) for device in every]
    onward = [(d, d ^ 2 if d % 2 else (d + 2) % sections) for d in every]
    return [
        ("near_query", "query", neighbours),
        *moves[:singles],
        ("near_own", "own", ring),
        *moves[singles:-1],
        ("even_query", "near_query", onward),
        moves[-1],
    ]


def packed(keys, values):
    return jnp.concatenate([jnp.transpose(keys, (1, 0, 2)), jnp.transpose(values, (1, 0, 2))])


def swapped_shards(
    queries, slice_own_keys, slice_own_values, cache_keys, context_value_rows, prefix_len
):
    groups = slice_own_keys.shape[1]
    sections = lax.axis_size("pipe")

    held = {
        "query": queries,
        "own": packed(slice_own_keys, slice_own_values),
        "m0": packed(cache_keys, context_value_rows),
    }
    for name, source, pairs in gather_plan(sections):
        held[name] = lax.ppermute(held[source], "pipe", pairs)
    blocks = [held[f"m{mask}"] for mask in range(sections)]
    return attend(
        prefix_len, held["even_query"], held["near_query"], held["near_own"], blocks, groups
    )


def solution(mesh):
    sections = mesh.shape["pipe"]
    unrolled = 4 <= sections <= unrolled_sections and sections & (sections - 1) == 0
    shards = swapped_shards if unrolled else gathered_shards
    in_specs = (
        P(("grp", "pipe"), "head", None),
        P(("grp", "pipe"), "head", None),
        P(("grp", "pipe"), "head", None),
        P(("grp", "pipe"), "head", None),
        P(("grp", "pipe"), "head", None),
        P("grp"),
    )
    out_specs = P(("grp", "pipe"), "head", None)
    return jax.shard_map(shards, mesh=mesh, in_specs=in_specs, out_specs=out_specs, check_vma=False)
```

```python
import functools
import math

import jax
import jax.numpy as jnp
from jax import lax
from jax.experimental import pallas as pl
from jax.experimental.pallas import tpu as pltpu
from jax.sharding import PartitionSpec as P


floor_value = -1e30
unrolled_sections = 16


def passed_along(value, axis, steps):
    count = lax.axis_size(axis)
    pairs = [(source, (source + steps) % count) for source in range(count)]
    return lax.ppermute(value, axis, pairs)


contract = (((1,), (1,)), ((), ()))


def own_prefix(prefix_ref):
    sections = prefix_ref.shape[1]
    section = lax.rem(lax.axis_index("pipe") + sections - 1, sections)
    column = lax.broadcasted_iota(jnp.int32, (1, sections), 1)
    prefix = jnp.where(column == section, prefix_ref[...].astype(jnp.float32), 0.0)
    return jnp.sum(prefix, axis=1, keepdims=True).astype(jnp.int32)


def visible_bias(prefix, masks, block_rows, extra):
    own_index = lax.axis_index("pipe")
    total = len(masks) * block_rows + extra
    position = lax.broadcasted_iota(jnp.int32, (1, total), 1)
    limit = jnp.full((1, total), total, jnp.int32)
    for slot, mask in enumerate(masks):
        first_key = lax.bitwise_xor(own_index, mask) * block_rows
        stop = jnp.minimum(prefix - first_key, block_rows) + slot * block_rows
        limit = jnp.where(position // block_rows == slot, stop, limit)
    return jnp.where(position < limit, 0.0, floor_value)


def joined_query(odd, heads, even_ref, odd_ref, ring_ref, slice_rows):
    relayed = jnp.where(odd, odd_ref[:, heads, :], even_ref[:, heads, :])
    rest = slice_rows - even_ref.shape[0]
    return jnp.concatenate([relayed, ring_ref[:rest, heads, :]], axis=0)


def early_kernel(scale, groups, masks, prefix_ref, even_ref, odd_ref, ring_ref, *refs):
    block_refs = dict(zip(masks, refs))
    weighted_ref, max_ref, sum_ref, hbm_ref, out_ref, sems = refs[len(masks):]
    own_index = lax.axis_index("pipe")
    odd = lax.rem(own_index, 2) == 1
    prefix = own_prefix(prefix_ref)
    slice_rows, head_count, head_width = out_ref.shape
    per_group = head_count // groups
    rows = slice_rows * per_group
    block_rows = block_refs[0].shape[1]
    rest = slice_rows - even_ref.shape[0]

    def part(group, masks, bias):
        heads = pl.ds(group * per_group, per_group)
        context = len(masks) * block_rows
        keys = [block_refs[mask][group] for mask in masks] + [ring_ref[rest + group]]
        values = [block_refs[mask][groups + group] for mask in masks] + [ring_ref[rest + groups + group]]
        query = joined_query(odd, heads, even_ref, odd_ref, ring_ref, slice_rows)
        scores = lax.dot_general(
            query.reshape(rows, head_width),
            jnp.concatenate(keys, axis=0),
            contract,
            preferred_element_type=jnp.float32,
        )
        key_index = lax.broadcasted_iota(jnp.int32, scores.shape, 1) - context
        row_index = lax.broadcasted_iota(jnp.int32, scores.shape, 0) // per_group
        scores = jnp.where(key_index <= row_index, scores + bias, floor_value)
        row_max = jnp.max(scores, axis=1, keepdims=True)
        weights = jnp.exp2((scores - row_max) * scale)
        total = jnp.sum(weights, axis=1, keepdims=True)
        weighted = jnp.dot(
            weights.astype(jnp.bfloat16),
            jnp.concatenate(values, axis=0),
            preferred_element_type=jnp.float32,
        )
        return weighted, row_max, total

    @pl.when(own_index == 0)
    def _():
        bias = visible_bias(prefix, masks[:1], block_rows, slice_rows)
        copies = []
        for group in range(groups):
            heads = pl.ds(group * per_group, per_group)
            weighted, _, total = part(group, masks[:1], bias)
            result = (weighted / total).astype(jnp.bfloat16)
            out_ref[:, heads, :] = result.reshape(slice_rows, per_group, head_width)
            copies.append(
                pltpu.make_async_copy(
                    out_ref.at[:, heads, :], hbm_ref.at[:, heads, :], sems.at[group]
                )
            )
            copies[-1].start()
        for copy in copies:
            copy.wait()

    @pl.when(own_index != 0)
    def _():
        bias = visible_bias(prefix, masks, block_rows, slice_rows)
        for group in range(groups):
            weighted, row_max, total = part(group, masks, bias)
            weighted_ref[group] = weighted
            max_ref[group] = jnp.broadcast_to(row_max, (rows, head_width))
            sum_ref[group] = jnp.broadcast_to(total, (rows, head_width))


def late_kernel(scale, groups, masks, prefix_ref, even_ref, odd_ref, ring_ref, *refs):
    block_refs = refs[: len(masks)]
    weighted_ref, max_ref, sum_ref, _, hbm_ref, out_ref, sems = refs[len(masks) :]
    own_index = lax.axis_index("pipe")
    odd = lax.rem(own_index, 2) == 1
    slice_rows, head_count, head_width = out_ref.shape
    per_group = head_count // groups
    rows = slice_rows * per_group
    block_rows = block_refs[0].shape[1]

    @pl.when(own_index != 0)
    def _():
        bias = visible_bias(own_prefix(prefix_ref), masks, block_rows, 0)
        copies = []
        for group in range(groups):
            heads = pl.ds(group * per_group, per_group)
            query = joined_query(odd, heads, even_ref, odd_ref, ring_ref, slice_rows)
            scores = bias + lax.dot_general(
                query.reshape(rows, head_width),
                jnp.concatenate([block_ref[group] for block_ref in block_refs], axis=0),
                contract,
                preferred_element_type=jnp.float32,
            )
            old_max = max_ref[group]
            new_max = jnp.maximum(old_max, jnp.max(scores, axis=1, keepdims=True))
            rescale = jnp.exp2((old_max - new_max) * scale)
            weights = jnp.exp2((scores - new_max[:, :1]) * scale)
            added = jnp.dot(
                weights.astype(jnp.bfloat16),
                jnp.concatenate([block_ref[groups + group] for block_ref in block_refs], axis=0),
                preferred_element_type=jnp.float32,
            )
            total = sum_ref[group] * rescale + jnp.sum(weights, axis=1, keepdims=True)
            result = ((weighted_ref[group] * rescale + added) / total).astype(jnp.bfloat16)
            out_ref[:, heads, :] = result.reshape(slice_rows, per_group, head_width)
            copies.append(
                pltpu.make_async_copy(
                    out_ref.at[:, heads, :], hbm_ref.at[:, heads, :], sems.at[group]
                )
            )
            copies[-1].start()
        for copy in copies:
            copy.wait()


def attend(prefix_len, even_query, odd_query, ring, blocks, late, shape, groups):
    slice_rows, head_count, head_width = shape
    rows = slice_rows * head_count
    vmem = pl.BlockSpec(memory_space=pltpu.VMEM)
    hbm = pl.BlockSpec(memory_space=pl.ANY)
    scale = math.log2(math.e) / math.sqrt(head_width)
    early = tuple(mask for mask in range(len(blocks)) if mask not in late)
    state = jax.ShapeDtypeStruct((groups, rows // groups, head_width), jnp.float32)
    out = jax.ShapeDtypeStruct(shape, jnp.bfloat16)
    scratch = [pltpu.VMEM(shape, jnp.bfloat16), pltpu.SemaphoreType.DMA((groups,))]
    params = pltpu.CompilerParams(vmem_limit_bytes=24 << 20)
    prefix = prefix_len.reshape(1, -1)

    def cost(masks):
        keys = len(masks) * blocks[0].shape[1]
        return pl.CostEstimate(
            flops=4 * keys * rows * head_width,
            bytes_accessed=4 * rows * head_width,
            transcendentals=keys * rows,
        )

    *partial, begun = pl.pallas_call(
        functools.partial(early_kernel, scale, groups, early),
        out_shape=(state, state, state, out),
        in_specs=[vmem] * (4 + len(early)),
        out_specs=(vmem, vmem, vmem, hbm),
        scratch_shapes=scratch,
        compiler_params=params,
        cost_estimate=cost(early),
        name="attend_early",
    )(prefix, even_query, odd_query, ring, *[blocks[mask] for mask in early])
    return pl.pallas_call(
        functools.partial(late_kernel, scale, groups, late),
        out_shape=out,
        in_specs=[vmem] * (7 + len(late)) + [hbm],
        out_specs=hbm,
        input_output_aliases={7 + len(late): 0},
        scratch_shapes=scratch,
        compiler_params=params,
        cost_estimate=cost(late),
        name="attend_late",
    )(prefix, even_query, odd_query, ring, *[blocks[mask] for mask in late], *partial, begun)


def block_scores(grouped, key_block, factor):
    return (
        jnp.einsum("sghd,kgd->gkhs", grouped, key_block, preferred_element_type=jnp.float32)
        * factor
    )


def to_rows(statistic):
    return jnp.transpose(statistic, (2, 0, 1))[..., None]


def absorb(running, scores, value_block, visible):
    weighted, running_max, running_sum = running
    block_max = jnp.max(jnp.where(visible, scores, floor_value), axis=1)
    new_max = jnp.maximum(running_max, block_max)
    weights = jnp.where(visible, jnp.exp(scores - new_max[:, None]), 0.0)
    rescale = jnp.exp(running_max - new_max)
    added = jnp.einsum(
        "gkhs,kgd->sghd",
        weights.astype(jnp.bfloat16),
        value_block,
        preferred_element_type=jnp.float32,
    )
    return (
        weighted * to_rows(rescale) + added,
        new_max,
        running_sum * rescale + jnp.sum(weights, axis=1),
    )


def cache_range(
    running, grouped, whole_keys, whole_values, start_key, stop_key, block_rows, factor
):

    def absorb_block(block_index, carried):
        first_key = block_index * block_rows
        key_block = lax.dynamic_slice_in_dim(whole_keys, first_key, block_rows, 0)
        value_block = lax.dynamic_slice_in_dim(whole_values, first_key, block_rows, 0)
        position = first_key + lax.broadcasted_iota(jnp.int32, (1, block_rows, 1, 1), 1)
        visible = (position >= start_key) & (position < stop_key)
        return absorb(carried, block_scores(grouped, key_block, factor), value_block, visible)

    return lax.fori_loop(
        start_key // block_rows, (stop_key + block_rows - 1) // block_rows, absorb_block, running
    )


def gathered_shards(
    queries, slice_own_keys, slice_own_values, cache_keys, context_value_rows, prefix_len
):
    slice_rows, head_count, head_width = queries.shape
    groups = slice_own_keys.shape[1]
    per_group = head_count // groups
    grouped = queries.reshape(slice_rows, groups, per_group, head_width)
    factor = 1.0 / math.sqrt(head_width)
    initial = (
        jnp.zeros((slice_rows, groups, per_group, head_width), jnp.float32),
        jnp.full((groups, per_group, slice_rows), floor_value, jnp.float32),
        jnp.zeros((groups, per_group, slice_rows), jnp.float32),
    )
    key_index = lax.broadcasted_iota(jnp.int32, (1, slice_rows, 1, slice_rows), 1)
    row_index = lax.broadcasted_iota(jnp.int32, (1, slice_rows, 1, slice_rows), 3)
    running = absorb(
        initial,
        block_scores(grouped, slice_own_keys, factor),
        slice_own_values,
        key_index <= row_index,
    )
    whole_keys = lax.all_gather(cache_keys, "pipe", axis=0, tiled=True)
    whole_values = lax.all_gather(context_value_rows, "pipe", axis=0, tiled=True)
    block_rows = math.gcd(whole_keys.shape[0], 512)
    own_prefix = prefix_len[lax.axis_index("pipe")]
    weighted, _, running_sum = cache_range(
        running, grouped, whole_keys, whole_values, 0, own_prefix, block_rows, factor
    )
    result = (weighted / to_rows(running_sum)).astype(jnp.bfloat16).reshape(queries.shape)
    return passed_along(result, "pipe", 1)


def gather_plan(sections):
    every = range(sections)
    moves = []
    for mask in sorted(range(1, sections), key=lambda mask: (mask.bit_count(), -mask)):
        swap = [(device, device ^ (mask & -mask)) for device in every]
        moves.append((f"m{mask}", f"m{mask & (mask - 1)}", swap))
    singles = sections.bit_length() - 1
    neighbours = [(device, device ^ 1) for device in every]
    ring = [(device, (device + 1) % sections) for device in every]
    onward = [(d, d ^ 2 if d % 2 else (d + 2) % sections) for d in every]
    return [
        moves[0],
        ("near_query", "query", neighbours),
        *moves[1:singles],
        ("ring", "rest", ring),
        *moves[singles:-2],
        ("even_query", "near_query", onward),
        *moves[-2:],
    ]


def packed(keys, values):
    return jnp.concatenate([jnp.transpose(keys, (1, 0, 2)), jnp.transpose(values, (1, 0, 2))])


def swapped_shards(
    queries, slice_own_keys, slice_own_values, cache_keys, context_value_rows, prefix_len
):
    groups = slice_own_keys.shape[1]
    sections = lax.axis_size("pipe")

    own = packed(slice_own_keys, slice_own_values)
    relayed = queries.shape[0] // 2
    late = (sections // 2 - 1, sections - 1)
    held = {
        "query": queries[:relayed],
        "rest": jnp.concatenate([queries[relayed:], own.reshape(-1, *queries.shape[1:])]),
        "m0": packed(cache_keys, context_value_rows),
    }
    for name, source, pairs in gather_plan(sections):
        held[name] = lax.ppermute(held[source], "pipe", pairs)
    blocks = [held[f"m{mask}"] for mask in range(sections)]
    return attend(
        prefix_len, held["even_query"], held["near_query"], held["ring"], blocks, late, queries.shape, groups
    )


def solution(mesh):
    sections = mesh.shape["pipe"]
    unrolled = 4 <= sections <= unrolled_sections and sections & (sections - 1) == 0
    shards = swapped_shards if unrolled else gathered_shards
    in_specs = (
        P(("grp", "pipe"), "head", None),
        P(("grp", "pipe"), "head", None),
        P(("grp", "pipe"), "head", None),
        P(("grp", "pipe"), "head", None),
        P(("grp", "pipe"), "head", None),
        P("grp"),
    )
    out_specs = P(("grp", "pipe"), "head", None)
    return jax.shard_map(shards, mesh=mesh, in_specs=in_specs, out_specs=out_specs, check_vma=False)
```
